256 devices in a mesh: rep: 16 (over y_hi, z), fsdp: 16 (over x, y_lo, core).
Axes of the slice: x: 4, y: 4 (y_hi: 2, y_lo: 2; y = y_hi * 2 + y_lo), z: 8, core: 2. Of those that a mesh axis runs over, the one named last changes fastest.
Arguments:
- tokens: bfloat16 [131072, 4096], P(('rep', 'fsdp')), may hold values from -6 to 6
- gate_pre: bfloat16 [131072, 768], P(('rep', 'fsdp')), may hold values from -8 to 8
- upstream: bfloat16 [131072, 768], P(('rep', 'fsdp')), may hold values from -6 to 6
- slow: float32 [16, 4096, 768], P('rep', 'fsdp'), may hold values from -6 to 6
- inner_mom: bfloat16 [16, 4096, 768], P('rep', 'fsdp'), may hold values from -6 to 6
- outer_mom: bfloat16 [16, 4096, 768], P('rep', 'fsdp'), may hold values from -3 to 3
- pairing: int32 [16], replicated, may hold values from 0 to 15, as said below
Outputs:
- gate_grad: bfloat16 [131072, 768], P(('rep', 'fsdp'))
- inner_new: bfloat16 [16, 4096, 768], P('rep', 'fsdp')
- outer_new: bfloat16 [16, 4096, 768], P('rep', 'fsdp')
- slow_new: float32 [16, 4096, 768], P('rep', 'fsdp')
The draws below stay inside these ranges and needn't reach their ends.
Inputs may be any that keep to these rules, and one draw needn't show every extreme that they name: pairing[i] = i XOR p for one p of 1 to 15 shared by all i, so pairing[pairing[i]] = i.
All inputs are finite; a program needn't handle non-finite values.
Results may differ from the reference program's by a relative error of at most 0.009.
Values may be sent and summed in bfloat16 or wider, within the bound.
No kernel may reach another device: no remote copies, remote signals or barrier semaphores. Data moves between devices by JAX's collectives and lax.ppermute only.
A program may use at most 128 MiB of HBM per device.

```python
import jax
import jax.numpy as jnp
from jax import lax

D = 4096
COLS = 768
GROUP_ROWS = 8192
TOKENS = 131072
N_REP = 16


def draw_pairing(key, part):
    partner_xor = jax.random.randint(jax.random.fold_in(key, 17), (), 1, N_REP, dtype=jnp.int32)
    return jnp.bitwise_xor(jnp.arange(N_REP, dtype=jnp.int32), partner_xor)


def block_scale(stream_key, extent, cuts, smallest, largest):
    factor_of = 1.0
    for position, shards_of in cuts:
        draws = jax.random.uniform(jax.random.fold_in(jax.random.fold_in(stream_key, 6), position), (shards_of,), jnp.float32, smallest / len(cuts), largest / len(cuts))
        factor_of = factor_of * jnp.repeat(jnp.exp(draws), extent[position] // shards_of).reshape((-1,) + (1,) * (len(extent) - 1 - position))
    return factor_of


def gaussian(key, extent, width, bound, split=(), kind=jnp.bfloat16):
    result = jax.random.normal(key, extent, jnp.float32) * width
    if len(split) > 0:
        result = block_scale(key, extent, split, -0.22, 0.18) * result
    return jnp.clip(result, min=-bound, max=bound).astype(kind)


def setup_inputs(seed: int = 0) -> dict:
    key_of = jax.random.split(jax.random.key(seed), 8)
    tokens = gaussian(key_of[0], (TOKENS, D), 1.0, 6.0, ((0, 256),))
    gate_pre = gaussian(key_of[1], (TOKENS, COLS), 1.5, 8.0, ((0, 256),))
    upstream = gaussian(key_of[2], (TOKENS, COLS), 1.0, 6.0, ((0, 256),))
    slow = gaussian(key_of[3], (N_REP, D, COLS), 1.0, 6.0, ((0, 16), (1, 16)), jnp.float32)
    inner_mom = gaussian(key_of[4], (N_REP, D, COLS), 1.0, 6.0, ((0, 16), (1, 16)))
    outer_mom = gaussian(key_of[5], (N_REP, D, COLS), 0.5, 3.0, ((0, 16), (1, 16)))
    pairing = draw_pairing(jax.random.fold_in(key_of[7], 71), 0)
    return {"tokens": tokens, "gate_pre": gate_pre, "upstream": upstream, "slow": slow, "inner_mom": inner_mom, "outer_mom": outer_mom, "pairing": pairing}


inner_beta = 0.9
inner_rate = 0.5
outer_mu = 0.9
outer_rate = 0.7


def reference(tokens, gate_pre, upstream, slow, inner_mom, outer_mom, pairing):
    weight_scale = float(D) ** -0.5
    token_blocks = tokens.reshape(N_REP, GROUP_ROWS, D)
    gate_blocks = gate_pre.reshape(N_REP, GROUP_ROWS, COLS)
    upstream_blocks = upstream.reshape(N_REP, GROUP_ROWS, COLS)
    fast_weight = slow.astype(jnp.bfloat16)

    def replica_pass(blocks):
        token_rows, gate_rows, upstream_rows, fast_block = blocks
        up_values = jnp.dot(token_rows, fast_block, preferred_element_type=jnp.float32) * weight_scale
        gate_values = gate_rows.astype(jnp.float32)
        sigmoid_gate = jax.nn.sigmoid(gate_values)
        upstream_values = upstream_rows.astype(jnp.float32)
        grad_rows = (upstream_values * gate_values * sigmoid_gate).astype(jnp.bfloat16)
        gate_grad = (upstream_values * up_values * sigmoid_gate * (1.0 + gate_values * (1.0 - sigmoid_gate))).astype(jnp.bfloat16)
        weight_grad = jnp.dot(token_rows.T, grad_rows, preferred_element_type=jnp.float32) * weight_scale
        return gate_grad, weight_grad

    gate_grad, weight_grad = lax.map(replica_pass, (token_blocks, gate_blocks, upstream_blocks, fast_weight))
    inner_new = (inner_beta * inner_mom.astype(jnp.float32) + weight_grad).astype(jnp.bfloat16)
    outer_grad = slow - (fast_weight.astype(jnp.float32) - inner_rate * inner_new.astype(jnp.float32))
    mean_slow = 0.5 * (slow + slow[pairing])
    mean_grad = 0.5 * (outer_grad + outer_grad[pairing])
    outer_new = (outer_mu * outer_mom.astype(jnp.float32) + mean_grad).astype(jnp.bfloat16)
    slow_new = mean_slow - outer_rate * (mean_grad + outer_mu * outer_new.astype(jnp.float32))
    return gate_grad.reshape(TOKENS, COLS), inner_new, outer_new, slow_new
```

```python
import jax
import jax.numpy as jnp
from jax import lax
from jax.sharding import Mesh, PartitionSpec as P

D = 4096
COLS = 768
HALF = COLS // 2
BLOCK = 256

inner_beta = 0.9
inner_rate = 0.5
outer_mu = 0.9
outer_rate = 0.7

F32 = jnp.float32
BF16 = jnp.bfloat16


def swap(block, axis):
    return lax.ppermute(block, axis, [(0, 1), (1, 0)])


def spread_x(block):
    return lax.all_to_all(block, "x", split_axis=0, concat_axis=0)


def pair_exchange(block, partner_xor):
    def branch(distance):
        route = [(i, i ^ distance) for i in range(16)]
        return lambda value: lax.ppermute(value, ("yh", "z"), route)

    return lax.switch(partner_xor - 1, [branch(d) for d in range(1, 16)], block)


def local(tokens, gate_pre, upstream, slow, inner_mom, outer_mom, pairing):
    weight_scale = float(D) ** (-0.5)
    first_core = lax.axis_index("core") == 0
    first_y = lax.axis_index("yl") == 0
    slow_shard = slow[0]
    fast_weight = slow_shard.astype(BF16)
    partner_xor = pairing[0]

    halves = tokens.reshape(512, 8, 2, BLOCK)
    even = halves[:, :, 0].reshape(512, 8 * BLOCK)
    odd = halves[:, :, 1].reshape(512, 8 * BLOCK)
    other_tokens = swap(jnp.where(first_core, odd, even), "core")
    own_tokens = jnp.where(first_core, even, odd)

    gate_values = gate_pre.astype(F32)
    sigmoid_gate = jax.nn.sigmoid(gate_values)
    upstream_values = upstream.astype(F32)
    grad_rows = (upstream_values * gate_values * sigmoid_gate).astype(BF16)
    other_grads = swap(grad_rows, "core")

    weight_a = fast_weight[:, :HALF]
    weight_b = fast_weight[:, HALF:]
    got = swap(weight_a, "yl")
    weight_a = jnp.where(first_y, jnp.stack([weight_a, got]), jnp.stack([got, weight_a]))
    weight_a = spread_x(jnp.broadcast_to(weight_a, (4, 2, BLOCK, HALF)))
    weight_b = spread_x(jnp.broadcast_to(weight_b, (4, BLOCK, HALF)))
    got = swap(weight_b, "yl")
    weight_b = jnp.where(
        first_y, jnp.stack([weight_b, got], 1), jnp.stack([got, weight_b], 1)
    )
    weight = jnp.concatenate(
        [weight_a.reshape(8 * BLOCK, HALF), weight_b.reshape(8 * BLOCK, HALF)], 1
    )

    contract_first = (((0,), (0,)), ((), ()))
    partial_grad = (
        lax.dot_general(own_tokens, grad_rows, contract_first, preferred_element_type=F32)
        + lax.dot_general(other_tokens, other_grads, contract_first, preferred_element_type=F32)
    ).astype(BF16)
    partial_grad = partial_grad.reshape(4, 2, BLOCK, COLS)

    part_a = jnp.sum(spread_x(partial_grad[..., :HALF]).astype(F32), 0)
    got = swap(jnp.where(first_y, part_a[1], part_a[0]).astype(BF16), "yl")
    part_a = jnp.where(first_y, part_a[0], part_a[1]) + got.astype(F32)
    part_b = partial_grad[..., HALF:]
    got = swap(jnp.where(first_y, part_b[:, 1], part_b[:, 0]), "yl")
    part_b = jnp.where(first_y, part_b[:, 0], part_b[:, 1]).astype(F32) + got.astype(F32)
    part_b = jnp.sum(spread_x(part_b.astype(BF16)).astype(F32), 0)
    weight_grad = jnp.concatenate([part_a, part_b], 1) * weight_scale

    inner_new = (inner_beta * inner_mom[0].astype(F32) + weight_grad).astype(BF16)
    outer_grad = slow_shard - (fast_weight.astype(F32) - inner_rate * inner_new.astype(F32))
    slow_partner = pair_exchange(fast_weight, partner_xor).astype(F32)
    grad_partner = pair_exchange(outer_grad.astype(BF16), partner_xor).astype(F32)
    mean_slow = 0.5 * (slow_shard + slow_partner)
    mean_grad = 0.5 * (outer_grad + grad_partner)
    outer_new = (outer_mu * outer_mom[0].astype(F32) + mean_grad).astype(BF16)
    slow_new = mean_slow - outer_rate * (mean_grad + outer_mu * outer_new.astype(F32))

    other_up = jnp.dot(other_tokens, weight, preferred_element_type=F32)
    own_up = jnp.dot(own_tokens, weight, preferred_element_type=F32)
    up_values = (own_up + swap(other_up, "core")) * weight_scale
    gate_grad = (
        upstream_values * up_values * sigmoid_gate * (1.0 + gate_values * (1.0 - sigmoid_gate))
    ).astype(BF16)
    return (gate_grad, inner_new[None], outer_new[None], slow_new[None])


def solution(mesh):
    fine = Mesh(mesh.devices.reshape(2, 8, 4, 2, 2), ("yh", "z", "x", "yl", "core"))
    rep, fsdp = ("yh", "z"), ("x", "yl", "core")
    rows = P(rep + fsdp, None)
    state = P(rep, fsdp, None)
    return jax.shard_map(
        local,
        mesh=fine,
        in_specs=(rows, rows, rows, state, state, state, P()),
        out_specs=(rows, state, state, state),
        check_vma=False,
    )
```

```python
import jax
import jax.numpy as jnp
from jax import lax
from jax.experimental import pallas as pl
from jax.experimental.pallas import tpu as pltpu
from jax.sharding import Mesh, PartitionSpec as P


D = 4096
COLS = 768
HALF = COLS // 2
BLOCK = 256
ROWS = 512

inner_beta = 0.9
inner_rate = 0.5
outer_mu = 0.9
outer_rate = 0.7

F32 = jnp.float32
BF16 = jnp.bfloat16
SHAPE = jax.ShapeDtypeStruct
WHOLE = pl.BlockSpec(memory_space=pltpu.VMEM)


def swap(block, axis):
    return lax.ppermute(block, axis, [(0, 1), (1, 0)])


def swap_x(block, distance):
    return lax.ppermute(block, "x", [(i, i ^ distance) for i in range(4)])


def pair_exchange(block, partner_xor):
    def branch(distance):
        route = [(i, i ^ distance) for i in range(16)]
        return lambda value: lax.ppermute(value, ("yh", "z"), route)

    return lax.switch(partner_xor - 1, [branch(d) for d in range(1, 16)], block)


def pick_kernel(order, tokens, out):
    out[...] = tokens[...]


def pick(tokens, order):
    return pl.pallas_call(
        pick_kernel,
        out_shape=SHAPE((ROWS, 8 * BLOCK), BF16),
        grid_spec=pltpu.PrefetchScalarGridSpec(
            num_scalar_prefetch=1,
            grid=(8,),
            in_specs=[pl.BlockSpec((ROWS, BLOCK), lambda i, order: (0, order[i]))],
            out_specs=pl.BlockSpec((ROWS, BLOCK), lambda i, order: (0, i)),
        ),
        cost_estimate=pl.CostEstimate(flops=0, bytes_accessed=2**22, transcendentals=0),
        name="pick",
    )(order, tokens)


def cast_kernel(slow, whole, first, second):
    fast = slow[...].astype(BF16)
    whole[...] = fast
    first[...] = fast[:, :HALF]
    second[...] = fast[:, HALF:]


def cast(slow):
    return pl.pallas_call(
        cast_kernel,
        out_shape=[SHAPE((BLOCK, COLS), BF16)] + [SHAPE((BLOCK, HALF), BF16)] * 2,
        in_specs=[WHOLE],
        out_specs=[WHOLE] * 3,
        cost_estimate=pl.CostEstimate(flops=0, bytes_accessed=2**20, transcendentals=0),
        name="cast",
    )(slow)


def grad_kernel(order, own_tokens, other_tokens, own_grads, other_grads, a0, a1, a2, a3, keep, send):
    step = pl.program_id(0)
    contract = (((0,), (0,)), ((), ()))
    total = lax.dot_general(
        own_tokens[...], own_grads[...], contract, preferred_element_type=F32
    ) + lax.dot_general(other_tokens[...], other_grads[...], contract, preferred_element_type=F32)
    total = total.astype(BF16)
    for distance, out in enumerate((a0, a1, a2, a3)):

        @pl.when(step // 2 == distance)
        def _():
            out[...] = total[:, :HALF]

    for side, out in enumerate((keep, send)):

        @pl.when(lax.rem(step, 2) == side)
        def _():
            out[...] = total[:, HALF:]


def partial_gradient(order, tokens, other_tokens, own_grads, other_grads):
    def piece(distance):
        return pl.BlockSpec(
            (BLOCK, HALF),
            lambda i, order: (jnp.clip(i - 2 * distance, 0, 1), 0),
        )

    grads = pl.BlockSpec((ROWS, COLS), lambda i, order: (0, 0))
    return pl.pallas_call(
        grad_kernel,
        out_shape=[SHAPE((2 * BLOCK, HALF), BF16)] * 4 + [SHAPE((4 * BLOCK, HALF), BF16)] * 2,
        grid_spec=pltpu.PrefetchScalarGridSpec(
            num_scalar_prefetch=1,
            grid=(8,),
            in_specs=[
                pl.BlockSpec((ROWS, BLOCK), lambda i, order: (0, order[i])),
                pl.BlockSpec((ROWS, BLOCK), lambda i, order: (0, i)),
                grads,
                grads,
            ],
            out_specs=[piece(distance) for distance in range(4)]
            + [
                pl.BlockSpec((BLOCK, HALF), lambda i, order: (i // 2, 0)),
                pl.BlockSpec((BLOCK, HALF), lambda i, order: (jnp.maximum(i - 1, 0) // 2, 0)),
            ],
        ),
        cost_estimate=pl.CostEstimate(
            flops=2 * 1024 * 2048 * 768, bytes_accessed=9 * 2**20, transcendentals=0
        ),
        name="weight_gradient",
    )(order, tokens, other_tokens, own_grads, other_grads)


def up_kernel(tokens, pair, x1, x2, x3, near, far, out):
    rows = 128

    @pl.loop(0, ROWS // rows)
    def _(tile):
        here = pl.ds(pl.multiple_of(tile * rows, rows), rows)

        def times(step, count, weight):
            return jnp.dot(
                tokens[here, step * BLOCK : (step + count) * BLOCK],
                weight,
                preferred_element_type=F32,
            )

        total = jnp.zeros((rows, HALF), F32)
        for distance, weight in enumerate((pair, x1, x2, x3)):
            total += times(2 * distance, 2, weight[...])
        out[here, :HALF] = total
        total = jnp.zeros((rows, HALF), F32)
        for side, weight in enumerate((near, far)):
            for distance in range(4):
                total += times(
                    2 * distance + side, 1, weight[distance * BLOCK : (distance + 1) * BLOCK, :]
                )
        out[here, HALF:] = total


def up_partial(tokens, *weights):
    return pl.pallas_call(
        up_kernel,
        out_shape=SHAPE((ROWS, COLS), F32),
        in_specs=[WHOLE] * 7,
        out_specs=WHOLE,
        cost_estimate=pl.CostEstimate(
            flops=2 * 512 * 2048 * 768, bytes_accessed=6 * 2**20, transcendentals=0
        ),
        name="up",
    )(tokens, *weights)


def local(tokens, gate_pre, upstream, slow, inner_mom, outer_mom, pairing):
    weight_scale = float(D) ** (-0.5)
    core = lax.axis_index("core")
    step = jnp.arange(8, dtype=jnp.int32)
    owner = (lax.axis_index("x") ^ (step // 2)) * 2 + (lax.axis_index("yl") ^ (step % 2))
    own_order = owner * 2 + core
    other_order = owner * 2 + (1 - core)
    slow_shard = slow[0]
    fast_weight, weight_a, weight_b = cast(slow_shard)
    partner_xor = pairing[0]

    other_tokens = swap(pick(tokens, other_order), "core")
    own_tokens = pick(tokens, own_order)

    gate_values = gate_pre.astype(F32)
    sigmoid_gate = jax.nn.sigmoid(gate_values)
    upstream_values = upstream.astype(F32)
    grad_rows = (upstream_values * gate_values * sigmoid_gate).astype(BF16)
    factor = (
        upstream_values * sigmoid_gate * (1.0 + gate_values * (1.0 - sigmoid_gate)) * weight_scale
    )
    grad_rows, factor = lax.optimization_barrier((grad_rows, factor))
    other_grads = swap(grad_rows, "core")

    pair = jnp.concatenate([weight_a, swap(weight_a, "yl")])
    near = jnp.concatenate([weight_b] + [swap_x(weight_b, k) for k in (1, 2, 3)])
    weights = [pair] + [swap_x(pair, k) for k in (1, 2, 3)] + [near, swap(near, "yl")]

    a0, a1, a2, a3, keep, send = partial_gradient(
        own_order, tokens, other_tokens, grad_rows, other_grads
    )
    part_a = a0.astype(F32)
    for k, piece in ((1, a1), (2, a2), (3, a3)):
        part_a = part_a + swap_x(piece, k).astype(F32)
    part_a = part_a[:BLOCK] + swap(part_a[BLOCK:].astype(BF16), "yl").astype(F32)
    part_b = keep.astype(F32) + swap(send, "yl").astype(F32)
    part_b = part_b.reshape(4, BLOCK, HALF)
    total_b = part_b[0]
    for k in (1, 2, 3):
        total_b = total_b + swap_x(part_b[k].astype(BF16), k).astype(F32)
    weight_grad = jnp.concatenate([part_a, total_b], 1) * weight_scale

    inner_new = (inner_beta * inner_mom[0].astype(F32) + weight_grad).astype(BF16)
    outer_grad = slow_shard - (fast_weight.astype(F32) - inner_rate * inner_new.astype(F32))
    slow_partner = pair_exchange(fast_weight, partner_xor).astype(F32)
    grad_partner = pair_exchange(outer_grad.astype(BF16), partner_xor).astype(F32)
    mean_slow = 0.5 * (slow_shard + slow_partner)
    mean_grad = 0.5 * (outer_grad + grad_partner)
    outer_new = (outer_mu * outer_mom[0].astype(F32) + mean_grad).astype(BF16)
    slow_new = mean_slow - outer_rate * (mean_grad + outer_mu * outer_new.astype(F32))

    other_up = swap(up_partial(other_tokens, *weights), "core")
    own_up = up_partial(own_tokens, *weights)
    gate_grad = ((own_up + other_up) * factor).astype(BF16)
    return (gate_grad, inner_new[None], outer_new[None], slow_new[None])


def solution(mesh):
    fine = Mesh(mesh.devices.reshape(2, 8, 4, 2, 2), ("yh", "z", "x", "yl", "core"))
    rep, fsdp = ("yh", "z"), ("x", "yl", "core")
    rows = P(rep + fsdp, None)
    state = P(rep, fsdp, None)


    return jax.shard_map(
        local,
        mesh=fine,
        in_specs=(rows, rows, rows, state, state, state, P()),
        out_specs=(rows, state, state, state),
        check_vma=False,
    )
```

```python
import jax
import jax.numpy as jnp
from jax import lax
from jax.experimental import pallas as pl
from jax.experimental.pallas import tpu as pltpu
from jax.sharding import Mesh, PartitionSpec as P


D = 4096
COLS = 768
HALF = COLS // 2
BLOCK = 256
ROWS = 512

inner_beta = 0.9
inner_rate = 0.5
outer_mu = 0.9
outer_rate = 0.7

F32 = jnp.float32
BF16 = jnp.bfloat16
SHAPE = jax.ShapeDtypeStruct
WHOLE = pl.BlockSpec(memory_space=pltpu.VMEM)


def swap(block, axis):
    return lax.ppermute(block, axis, [(0, 1), (1, 0)])


def swap_x(block, distance):
    return lax.ppermute(block, "x", [(i, i ^ distance) for i in range(4)])


def pair_exchange(block, partner_xor):
    def branch(distance):
        route = [(i, i ^ distance) for i in range(16)]
        return lambda value: lax.ppermute(value, ("yh", "z"), route)

    return lax.switch(partner_xor - 1, [branch(d) for d in range(1, 16)], block)


def limits(mebibytes):
    return pltpu.CompilerParams(vmem_limit_bytes=mebibytes * 2**20)


def pick_kernel(tokens, other, own, sems):
    core = lax.axis_index("core")
    copies = []
    for which, (side, out) in enumerate(((1 - core, other), (core, own))):
        for step in range(8):
            x = lax.axis_index("x") ^ (step // 2)
            y = lax.axis_index("yl") ^ (step % 2)
            owner = (x * 2 + y) * 2 + side
            columns = pl.ds(pl.multiple_of(owner * BLOCK, BLOCK), BLOCK)
            copies.append(
                pltpu.make_async_copy(
                    tokens.at[:, columns],
                    out.at[:, step * BLOCK : (step + 1) * BLOCK],
                    sems.at[which, step],
                )
            )
    for copy in copies:
        copy.start()
    for copy in copies:
        copy.wait()


def pick(tokens):
    return pl.pallas_call(
        pick_kernel,
        out_shape=[SHAPE((ROWS, 8 * BLOCK), BF16)] * 2,
        in_specs=[pl.BlockSpec(memory_space=pl.ANY)],
        out_specs=[WHOLE] * 2,
        scratch_shapes=[pltpu.SemaphoreType.DMA((2, 8))],
        cost_estimate=pl.CostEstimate(flops=0, bytes_accessed=2**22, transcendentals=0),
        compiler_params=limits(58),
        name="pick",
    )(tokens)


def cast_kernel(slow, whole, first, second):
    fast = slow[...].astype(BF16)
    whole[...] = fast
    first[...] = fast[:, :HALF]
    second[...] = fast[:, HALF:]


def cast(slow):
    return pl.pallas_call(
        cast_kernel,
        out_shape=[SHAPE((BLOCK, COLS), BF16)] + [SHAPE((BLOCK, HALF), BF16)] * 2,
        in_specs=[WHOLE],
        out_specs=[WHOLE] * 3,
        cost_estimate=pl.CostEstimate(flops=0, bytes_accessed=2**20, transcendentals=0),
        compiler_params=limits(4),
        name="cast",
    )(slow)


def join_kernel(*refs):
    out = refs[-1]
    for place, part in enumerate(refs[:-1]):
        out[place * BLOCK : (place + 1) * BLOCK, :] = part[...]


def join(*parts):
    return pl.pallas_call(
        join_kernel,
        out_shape=SHAPE((len(parts) * BLOCK, HALF), BF16),
        in_specs=[WHOLE] * len(parts),
        out_specs=WHOLE,
        cost_estimate=pl.CostEstimate(flops=0, bytes_accessed=2**20, transcendentals=0),
        compiler_params=limits(4),
        name="join",
    )(*parts)


def grad_kernel(own_tokens, other_tokens, own_grads, other_grads, a0, a1, a2, a3, keep, send):
    contract = (((0,), (0,)), ((), ()))
    for step in range(8):
        distance, side = divmod(step, 2)
        columns = slice(step * BLOCK, (step + 1) * BLOCK)
        total = lax.dot_general(
            own_tokens[:, columns], own_grads[...], contract, preferred_element_type=F32
        ) + lax.dot_general(
            other_tokens[:, columns], other_grads[...], contract, preferred_element_type=F32
        )
        total = total.astype(BF16)
        (a0, a1, a2, a3)[distance][side * BLOCK : (side + 1) * BLOCK, :] = total[:, :HALF]
        (keep, send)[side][distance * BLOCK : (distance + 1) * BLOCK, :] = total[:, HALF:]


def partial_gradient(own_tokens, other_tokens, own_grads, other_grads):
    return pl.pallas_call(
        grad_kernel,
        out_shape=[SHAPE((2 * BLOCK, HALF), BF16)] * 4 + [SHAPE((4 * BLOCK, HALF), BF16)] * 2,
        in_specs=[WHOLE] * 4,
        out_specs=[WHOLE] * 6,
        cost_estimate=pl.CostEstimate(
            flops=2 * 1024 * 2048 * 768, bytes_accessed=9 * 2**20, transcendentals=0
        ),
        compiler_params=limits(14),
        name="weight_gradient",
    )(own_tokens, other_tokens, own_grads, other_grads)


def up_kernel(tokens, pair, x1, x2, x3, near, far, out):
    rows = 128

    @pl.loop(0, ROWS // rows)
    def _(tile):
        here = pl.ds(pl.multiple_of(tile * rows, rows), rows)

        def times(step, count, weight):
            return jnp.dot(
                tokens[here, step * BLOCK : (step + count) * BLOCK],
                weight,
                preferred_element_type=F32,
            )

        total = jnp.zeros((rows, HALF), F32)
        for distance, weight in enumerate((pair, x1, x2, x3)):
            total += times(2 * distance, 2, weight[...])
        out[here, :HALF] = total
        total = jnp.zeros((rows, HALF), F32)
        for side, weight in enumerate((near, far)):
            for distance in range(4):
                total += times(
                    2 * distance + side, 1, weight[distance * BLOCK : (distance + 1) * BLOCK, :]
                )
        out[here, HALF:] = total


def up_partial(tokens, *weights):
    return pl.pallas_call(
        up_kernel,
        out_shape=SHAPE((ROWS, COLS), F32),
        in_specs=[WHOLE] * 7,
        out_specs=WHOLE,
        cost_estimate=pl.CostEstimate(
            flops=2 * 512 * 2048 * 768, bytes_accessed=6 * 2**20, transcendentals=0
        ),
        compiler_params=limits(12),
        name="up",
    )(tokens, *weights)


def inner_kernel(part_a, part_b, got_a, b1, b2, b3, inner_mom, slow, fast, inner_new, outer_grad):
    scale = float(D) ** (-0.5)
    total_b = part_b[...]
    for got in (b1, b2, b3):
        total_b += got[...].astype(F32)
    for here, total in (
        (slice(0, HALF), part_a[...] + got_a[...].astype(F32)),
        (slice(HALF, COLS), total_b),
    ):
        inner = (inner_beta * inner_mom[:, here].astype(F32) + total * scale).astype(BF16)
        inner_new[:, here] = inner
        outer_grad[:, here] = (
            slow[:, here] - (fast[:, here].astype(F32) - inner_rate * inner.astype(F32))
        ).astype(BF16)


def inner_update(*operands):
    return pl.pallas_call(
        inner_kernel,
        out_shape=[SHAPE((BLOCK, COLS), BF16)] * 2,
        in_specs=[WHOLE] * 9,
        out_specs=[WHOLE] * 2,
        cost_estimate=pl.CostEstimate(flops=0, bytes_accessed=2**21, transcendentals=0),
        compiler_params=limits(8),
        name="inner",
    )(*operands)


def outer_kernel(slow, fast, inner_new, slow_partner, grad_partner, outer_mom, outer_new, slow_new):
    slow_values = slow[...]
    outer_grad = slow_values - (
        fast[...].astype(F32) - inner_rate * inner_new[...].astype(F32)
    )
    mean_slow = 0.5 * (slow_values + slow_partner[...].astype(F32))
    mean_grad = 0.5 * (outer_grad + grad_partner[...].astype(F32))
    outer = (outer_mu * outer_mom[...].astype(F32) + mean_grad).astype(BF16)
    outer_new[...] = outer
    slow_new[...] = mean_slow - outer_rate * (mean_grad + outer_mu * outer.astype(F32))


def outer_update(*operands):
    return pl.pallas_call(
        outer_kernel,
        out_shape=[SHAPE((BLOCK, COLS), BF16), SHAPE((BLOCK, COLS), F32)],
        in_specs=[WHOLE] * 6,
        out_specs=[WHOLE] * 2,
        cost_estimate=pl.CostEstimate(flops=0, bytes_accessed=2**21, transcendentals=0),
        compiler_params=limits(8),
        name="outer",
    )(*operands)


def local(tokens, gate_pre, upstream, slow, inner_mom, outer_mom, pairing):
    weight_scale = float(D) ** (-0.5)
    slow_shard = slow[0]
    fast_weight, weight_a, weight_b = cast(slow_shard)
    partner_xor = pairing[0]

    other_tokens, own_tokens = pick(tokens)
    other_tokens = swap(other_tokens, "core")

    gate_values = gate_pre.astype(F32)
    sigmoid_gate = jax.nn.sigmoid(gate_values)
    upstream_values = upstream.astype(F32)
    grad_rows = (upstream_values * gate_values * sigmoid_gate).astype(BF16)
    factor = (
        upstream_values * sigmoid_gate * (1.0 + gate_values * (1.0 - sigmoid_gate)) * weight_scale
    )
    grad_rows, factor = lax.optimization_barrier((grad_rows, factor))
    other_grads = swap(grad_rows, "core")

    pair = join(weight_a, swap(weight_a, "yl"))
    near = join(weight_b, *[swap_x(weight_b, k) for k in (1, 2, 3)])
    weights = [pair] + [swap_x(pair, k) for k in (1, 2, 3)] + [near, swap(near, "yl")]

    a0, a1, a2, a3, keep, send = partial_gradient(
        own_tokens, other_tokens, grad_rows, other_grads
    )
    part_a = a0.astype(F32)
    for k, piece in ((1, a1), (2, a2), (3, a3)):
        part_a = part_a + swap_x(piece, k).astype(F32)
    got_a = swap(part_a[BLOCK:].astype(BF16), "yl")
    part_b = keep.astype(F32) + swap(send, "yl").astype(F32)
    part_b = part_b.reshape(4, BLOCK, HALF)
    got_b = [swap_x(part_b[k].astype(BF16), k) for k in (1, 2, 3)]
    inner_new, outer_grad = inner_update(
        part_a[:BLOCK], part_b[0], got_a, *got_b, inner_mom[0], slow_shard, fast_weight
    )
    slow_partner = pair_exchange(fast_weight, partner_xor)
    grad_partner = pair_exchange(outer_grad, partner_xor)
    outer_new, slow_new = outer_update(
        slow_shard, fast_weight, inner_new, slow_partner, grad_partner, outer_mom[0]
    )

    other_up = up_partial(other_tokens, *weights)
    own_up = up_partial(own_tokens, *weights)
    other_up = swap(other_up, "core")
    gate_grad = ((own_up + other_up) * factor).astype(BF16)
    return (gate_grad, inner_new[None], outer_new[None], slow_new[None])


def solution(mesh):
    fine = Mesh(mesh.devices.reshape(2, 8, 4, 2, 2), ("yh", "z", "x", "yl", "core"))
    rep, fsdp = ("yh", "z"), ("x", "yl", "core")
    rows = P(rep + fsdp, None)
    state = P(rep, fsdp, None)


    return jax.shard_map(
        local,
        mesh=fine,
        in_specs=(rows, rows, rows, state, state, state, P()),
        out_specs=(rows, state, state, state),
        check_vma=False,
    )
```

```python
import jax
import jax.numpy as jnp
from jax import lax
from jax.experimental import pallas as pl
from jax.experimental.pallas import tpu as pltpu
from jax.sharding import Mesh, PartitionSpec as P


D = 4096
COLS = 768
HALF = COLS // 2
BLOCK = 256
ROWS = 512

inner_beta = 0.9
inner_rate = 0.5
outer_mu = 0.9
outer_rate = 0.7

F32 = jnp.float32
BF16 = jnp.bfloat16
SHAPE = jax.ShapeDtypeStruct
WHOLE = pl.BlockSpec(memory_space=pltpu.VMEM)


def swap(block, axis):
    return lax.ppermute(block, axis, [(0, 1), (1, 0)])


def swap_x(block, distance):
    return lax.ppermute(block, "x", [(i, i ^ distance) for i in range(4)])


def pair_exchange(block, partner_xor):
    def branch(distance):
        route = [(i, i ^ distance) for i in range(16)]
        return lambda value: lax.ppermute(value, ("yh", "z"), route)

    return lax.switch(partner_xor - 1, [branch(d) for d in range(1, 16)], block)


def limits(mebibytes):
    return pltpu.CompilerParams(vmem_limit_bytes=mebibytes * 2**20)


def pick_kernel(tokens, other, own, sems):
    core = lax.axis_index("core")
    copies = []
    for which, (side, out) in enumerate(((1 - core, other), (core, own))):
        for step in range(8):
            x = lax.axis_index("x") ^ (step // 2)
            y = lax.axis_index("yl") ^ (step % 2)
            owner = (x * 2 + y) * 2 + side
            columns = pl.ds(pl.multiple_of(owner * BLOCK, BLOCK), BLOCK)
            copies.append(
                pltpu.make_async_copy(
                    tokens.at[:, columns],
                    out.at[:, step * BLOCK : (step + 1) * BLOCK],
                    sems.at[which, step],
                )
            )
    for copy in copies:
        copy.start()
    for copy in copies:
        copy.wait()


def pick(tokens):
    return pl.pallas_call(
        pick_kernel,
        out_shape=[SHAPE((ROWS, 8 * BLOCK), BF16)] * 2,
        in_specs=[pl.BlockSpec(memory_space=pl.ANY)],
        out_specs=[WHOLE] * 2,
        scratch_shapes=[pltpu.SemaphoreType.DMA((2, 8))],
        cost_estimate=pl.CostEstimate(flops=0, bytes_accessed=2**22, transcendentals=0),
        compiler_params=limits(46),
        name="pick",
    )(tokens)


def cast_kernel(slow, whole, first, second):
    fast = slow[...].astype(BF16)
    whole[...] = fast
    first[...] = fast[:, :HALF]
    second[...] = fast[:, HALF:]


def cast(slow):
    return pl.pallas_call(
        cast_kernel,
        out_shape=[SHAPE((BLOCK, COLS), BF16)] + [SHAPE((BLOCK, HALF), BF16)] * 2,
        in_specs=[WHOLE],
        out_specs=[WHOLE] * 3,
        cost_estimate=pl.CostEstimate(flops=0, bytes_accessed=2**20, transcendentals=0),
        compiler_params=limits(4),
        name="cast",
    )(slow)


def join_kernel(*refs):
    out = refs[-1]
    for place, part in enumerate(refs[:-1]):
        out[place * BLOCK : (place + 1) * BLOCK, :] = part[...]


def join(*parts):
    return pl.pallas_call(
        join_kernel,
        out_shape=SHAPE((len(parts) * BLOCK, HALF), BF16),
        in_specs=[WHOLE] * len(parts),
        out_specs=WHOLE,
        cost_estimate=pl.CostEstimate(flops=0, bytes_accessed=2**20, transcendentals=0),
        compiler_params=limits(4),
        name="join",
    )(*parts)


def grad_kernel(own_tokens, other_tokens, own_grads, other_grads, a0, a1, a2, a3, keep, send):
    contract = (((0,), (0,)), ((), ()))
    for step in range(8):
        distance, side = divmod(step, 2)
        columns = slice(step * BLOCK, (step + 1) * BLOCK)
        total = lax.dot_general(
            own_tokens[:, columns], own_grads[...], contract, preferred_element_type=F32
        ) + lax.dot_general(
            other_tokens[:, columns], other_grads[...], contract, preferred_element_type=F32
        )
        total = total.astype(BF16)
        (a0, a1, a2, a3)[distance][side * BLOCK : (side + 1) * BLOCK, :] = total[:, :HALF]
        (keep, send)[side][distance * BLOCK : (distance + 1) * BLOCK, :] = total[:, HALF:]


def partial_gradient(own_tokens, other_tokens, own_grads, other_grads):
    return pl.pallas_call(
        grad_kernel,
        out_shape=[SHAPE((2 * BLOCK, HALF), BF16)] * 4 + [SHAPE((4 * BLOCK, HALF), BF16)] * 2,
        in_specs=[WHOLE] * 4,
        out_specs=[WHOLE] * 6,
        cost_estimate=pl.CostEstimate(
            flops=2 * 1024 * 2048 * 768, bytes_accessed=9 * 2**20, transcendentals=0
        ),
        compiler_params=limits(14),
        name="weight_gradient",
    )(own_tokens, other_tokens, own_grads, other_grads)


def up_first_kernel(tokens, *refs):
    pieces, out, weight, partial, sems = refs[:6], *refs[6:]
    halves = []
    for half in range(2):
        copies = []
        for k in (2 * half, 2 * half + 1):
            copies.append((pieces[k], weight.at[2 * k * BLOCK : (2 * k + 2) * BLOCK, 0:HALF]))
            for side in range(2):
                place = (2 * k + side) * BLOCK
                copies.append(
                    (
                        pieces[4 + side].at[k * BLOCK : (k + 1) * BLOCK],
                        weight.at[place : place + BLOCK, HALF:COLS],
                    )
                )
        halves.append(
            [
                pltpu.make_async_copy(source, target, sems.at[half, place])
                for place, (source, target) in enumerate(copies)
            ]
        )
    for copy in halves[0] + halves[1]:
        copy.start()
    depth = 4 * BLOCK
    for copy in halves[0]:
        copy.wait()
    partial[...] = jnp.dot(tokens[:, :depth], weight[:depth, :], preferred_element_type=F32)
    for copy in halves[1]:
        copy.wait()
    out[...] = (
        partial[...]
        + jnp.dot(tokens[:, depth:], weight[depth:, :], preferred_element_type=F32)
    ).astype(BF16)


def up_first(tokens, *pieces):
    return pl.pallas_call(
        up_first_kernel,
        out_shape=[SHAPE((ROWS, COLS), BF16), SHAPE((8 * BLOCK, COLS), BF16)],
        in_specs=[WHOLE] + [pl.BlockSpec(memory_space=pl.ANY)] * 6,
        out_specs=[WHOLE] * 2,
        scratch_shapes=[pltpu.VMEM((ROWS, COLS), F32), pltpu.SemaphoreType.DMA((2, 6))],
        cost_estimate=pl.CostEstimate(
            flops=2 * 512 * 2048 * 768, bytes_accessed=6 * 2**20, transcendentals=0
        ),
        compiler_params=limits(14),
        name="up_first",
    )(tokens, *pieces)


def up_second_kernel(tokens, weight, out):
    out[...] = jnp.dot(tokens[...], weight[...], preferred_element_type=F32)


def up_second(tokens, weight):
    return pl.pallas_call(
        up_second_kernel,
        out_shape=SHAPE((ROWS, COLS), F32),
        in_specs=[WHOLE] * 2,
        out_specs=WHOLE,
        cost_estimate=pl.CostEstimate(
            flops=2 * 512 * 2048 * 768, bytes_accessed=6 * 2**20, transcendentals=0
        ),
        compiler_params=limits(10),
        name="up_second",
    )(tokens, weight)


def inner_kernel(part_a, part_b, got_a, b1, b2, b3, inner_mom, slow, inner_new, outer_grad):
    scale = float(D) ** (-0.5)
    total_b = part_b[...]
    for got in (b1, b2, b3):
        total_b += got[...].astype(F32)
    for here, total in (
        (slice(0, HALF), part_a[...] + got_a[...].astype(F32)),
        (slice(HALF, COLS), total_b),
    ):
        inner = (inner_beta * inner_mom[:, here].astype(F32) + total * scale).astype(BF16)
        inner_new[:, here] = inner
        slow_values = slow[:, here]
        fast_values = slow_values.astype(BF16).astype(F32)
        outer_grad[:, here] = (
            slow_values - (fast_values - inner_rate * inner.astype(F32))
        ).astype(BF16)


def inner_update(*operands):
    return pl.pallas_call(
        inner_kernel,
        out_shape=[SHAPE((BLOCK, COLS), BF16)] * 2,
        in_specs=[WHOLE] * 8,
        out_specs=[WHOLE] * 2,
        cost_estimate=pl.CostEstimate(flops=0, bytes_accessed=2**21, transcendentals=0),
        compiler_params=limits(8),
        name="inner",
    )(*operands)


def outer_kernel(slow, inner_new, slow_partner, grad_partner, outer_mom, outer_new, slow_new):
    slow_values = slow[...]
    outer_grad = slow_values - (
        slow_values.astype(BF16).astype(F32) - inner_rate * inner_new[...].astype(F32)
    )
    mean_slow = 0.5 * (slow_values + slow_partner[...].astype(F32))
    mean_grad = 0.5 * (outer_grad + grad_partner[...].astype(F32))
    outer = (outer_mu * outer_mom[...].astype(F32) + mean_grad).astype(BF16)
    outer_new[...] = outer
    slow_new[...] = mean_slow - outer_rate * (mean_grad + outer_mu * outer.astype(F32))


def outer_update(*operands):
    return pl.pallas_call(
        outer_kernel,
        out_shape=[SHAPE((BLOCK, COLS), BF16), SHAPE((BLOCK, COLS), F32)],
        in_specs=[WHOLE] * 5,
        out_specs=[WHOLE] * 2,
        cost_estimate=pl.CostEstimate(flops=0, bytes_accessed=2**21, transcendentals=0),
        compiler_params=limits(8),
        name="outer",
    )(*operands)


def local(tokens, gate_pre, upstream, slow, inner_mom, outer_mom, pairing):
    weight_scale = float(D) ** (-0.5)
    slow_shard = slow[0]
    fast_weight, weight_a, weight_b = cast(slow_shard)
    partner_xor = pairing[0]

    other_tokens, own_tokens = pick(tokens)
    other_tokens = swap(other_tokens, "core")

    gate_values = gate_pre.astype(F32)
    sigmoid_gate = jax.nn.sigmoid(gate_values)
    upstream_values = upstream.astype(F32)
    grad_rows = (upstream_values * gate_values * sigmoid_gate).astype(BF16)
    factor = (
        upstream_values * sigmoid_gate * (1.0 + gate_values * (1.0 - sigmoid_gate)) * weight_scale
    )
    grad_rows, factor = lax.optimization_barrier((grad_rows, factor))
    other_grads = swap(grad_rows, "core")

    pair = join(weight_a, swap(weight_a, "yl"))
    near = join(weight_b, *[swap_x(weight_b, k) for k in (1, 2, 3)])
    weights = [pair] + [swap_x(pair, k) for k in (1, 2, 3)] + [near, swap(near, "yl")]

    a0, a1, a2, a3, keep, send = partial_gradient(
        own_tokens, other_tokens, grad_rows, other_grads
    )
    part_a = a0.astype(F32)
    for k, piece in ((1, a1), (2, a2), (3, a3)):
        part_a = part_a + swap_x(piece, k).astype(F32)
    got_a = swap(part_a[BLOCK:].astype(BF16), "yl")
    part_b = keep.astype(F32) + swap(send, "yl").astype(F32)
    part_b = part_b.reshape(4, BLOCK, HALF)
    got_b = [swap_x(part_b[k].astype(BF16), k) for k in (1, 2, 3)]
    inner_new, outer_grad = inner_update(
        part_a[:BLOCK], part_b[0], got_a, *got_b, inner_mom[0], slow_shard
    )
    slow_partner = pair_exchange(fast_weight, partner_xor)
    grad_partner = pair_exchange(outer_grad, partner_xor)
    outer_new, slow_new = outer_update(
        slow_shard, inner_new, slow_partner, grad_partner, outer_mom[0]
    )

    other_up, weight = up_first(other_tokens, *weights)
    other_up = swap(other_up, "core")
    own_up = up_second(own_tokens, weight)
    gate_grad = ((own_up + other_up.astype(F32)) * factor).astype(BF16)
    return (gate_grad, inner_new[None], outer_new[None], slow_new[None])


def solution(mesh):
    fine = Mesh(mesh.devices.reshape(2, 8, 4, 2, 2), ("yh", "z", "x", "yl", "core"))
    rep, fsdp = ("yh", "z"), ("x", "yl", "core")
    rows = P(rep + fsdp, None)
    state = P(rep, fsdp, None)


    return jax.shard_map(
        local,
        mesh=fine,
        in_specs=(rows, rows, rows, state, state, state, P()),
        out_specs=(rows, state, state, state),
        check_vma=False,
    )
```
